32 devices in a mesh: row: 8 (over y, x, core), col: 4 (over z).
Axes of the slice: x: 2, y: 2, z: 4, core: 2. Of those that a mesh axis runs over, the one named last changes fastest.
Arguments:
- inverse: float32 [4096, 4096], P('row', 'col'), may hold values from -0.05 to 0.05
- owner: int32 [32], replicated, may hold values from 0 to 31, each once
- struct_parent: int32 [32], replicated, may hold values 0 or 1
- struct_child: int32 [32], replicated, may hold values 0 or 1
- panel_parent: float32 [4096, 1024], P('row', 'col'), may hold values from -1.5 to 1.5
- panel_child: float32 [4096, 1024], P('row', 'col'), may hold values from -1.5 to 1.5
- child_on_parent: float32 [1024, 1024], P('col'), may hold values from -0.1875 to 0.1875
- dinv_parent: float32 [1024, 1024], P('col'), may hold values from -6 to 6
- dinv_child: float32 [1024, 1024], P('col'), may hold values from -6 to 6
Outputs:
- row_parent: float32 [1024, 4096], P('col', 'row')
- inv_parent: float32 [1024, 1024], P('col')
- row_child: float32 [1024, 4096], P('col', 'row')
- inv_cross: float32 [1024, 1024], P('col')
- inv_child: float32 [1024, 1024], P('col')
The draws below stay inside these ranges and needn't reach their ends.
Inputs may be any that keep to these rules, and one draw needn't show every extreme that they name: `owner`: each slot holds a different block.
All inputs are finite; a program needn't handle non-finite values.
Results may differ from the reference program's by a relative error of at most 0.000071.
Values sent between devices are 32-bit elements; how exact they have to be, the bound alone decides.
A program may use at most 128 MiB of HBM per device.

```python
import jax
import jax.numpy as jnp
from jax import lax

W = 1024
BLOCK_ROWS = 128
M = 4096
NBLK = 32


def touch_ends(drawn, rng, least, largest):
    index_at = [jax.random.randint(jax.random.fold_in(rng, axis), (), 0, length) for axis, length in enumerate(drawn.shape)]
    main_axis = drawn.shape.index(max(drawn.shape))
    next_to = index_at[:main_axis] + [(index_at[main_axis] + 1) % drawn.shape[main_axis]] + index_at[main_axis + 1:]
    return drawn.at[tuple(index_at)].set(least).at[tuple(next_to)].set(largest)


def shard_levels(stream_key, shape, pieces, least, high):
    gain, own = 1.0, jax.random.fold_in(stream_key, 6)
    for dim, blocks in pieces:
        heights = jnp.exp(jax.random.uniform(jax.random.fold_in(own, dim), (blocks,), jnp.float32, least / len(pieces), high / len(pieces)))
        gain = gain * jnp.repeat(heights, shape[dim] // blocks).reshape([-1 if axis == dim else 1 for axis in range(len(shape))])
    return gain


def centred(rng, dims, spread, reach, cuts=(), kind=jnp.bfloat16):
    factor_of = shard_levels(rng, dims, cuts, -0.22, 0.18) if cuts else 1.0
    array = jax.random.normal(rng, dims, jnp.float32) * spread * factor_of
    return jnp.minimum(jnp.maximum(array, -reach), reach).astype(kind)


def setup_inputs(seed: int = 0) -> dict:
    key_list = jax.random.split(jax.random.key(seed), 10)
    return {
        "inverse": centred(key_list[0], (M, M), 0.008, 0.05, ((0, 8), (1, 4)), jnp.float32),
        "owner": jax.random.permutation(key_list[1], NBLK).astype(jnp.int32),
        "struct_parent": touch_ends((jax.random.randint(key_list[2], (NBLK,), 0, 4) < 3).astype(jnp.int32), jax.random.fold_in(key_list[2], 1), 0, 1),
        "struct_child": touch_ends((jax.random.randint(key_list[3], (NBLK,), 0, 4) < 3).astype(jnp.int32), jax.random.fold_in(key_list[3], 1), 0, 1),
        "panel_parent": centred(key_list[4], (M, W), 0.25, 1.5, ((0, 8), (1, 4)), jnp.float32),
        "panel_child": centred(key_list[5], (M, W), 0.25, 1.5, ((0, 8), (1, 4)), jnp.float32),
        "child_on_parent": centred(key_list[6], (W, W), W ** -0.5, 0.1875, ((0, 4),), jnp.float32),
        "dinv_parent": centred(key_list[7], (W, W), 1.0, 6.0, ((0, 4),), jnp.float32),
        "dinv_child": centred(key_list[8], (W, W), 1.0, 6.0, ((0, 4),), jnp.float32),
    }


def slot_mask(struct, owner):
    live = struct[owner].astype(jnp.float32)
    return jnp.repeat(live, BLOCK_ROWS)


def matmul(left, right):
    return jnp.dot(left, right, precision=lax.Precision.HIGHEST, preferred_element_type=jnp.float32)


def reference(inverse, owner, struct_parent, struct_child, panel_parent, panel_child, child_on_parent, dinv_parent, dinv_child):
    mask_parent = slot_mask(struct_parent, owner)
    mask_child = slot_mask(struct_parent * struct_child, owner)
    masked_parent = panel_parent * mask_parent[:, None]
    masked_child = panel_child * mask_child[:, None]
    row_parent = -matmul(inverse, masked_parent).T * mask_parent[None, :]
    inv_parent = dinv_parent - matmul(row_parent, masked_parent)
    row_child = -(matmul(inverse, masked_child).T + matmul(child_on_parent.T, row_parent)) * mask_child[None, :]
    inv_cross = -(matmul(row_parent, masked_child) + matmul(inv_parent, child_on_parent))
    inv_child = dinv_child - matmul(row_child, masked_child) - matmul(inv_cross.T, child_on_parent)
    return (row_parent, inv_parent, row_child, inv_cross, inv_child)
```

```python
import jax
import jax.numpy as jnp
from jax import lax
from jax.sharding import PartitionSpec as P

BLOCK_ROWS = 128
PRECISION = lax.Precision.HIGH


def contract(left, right, left_dim, right_dim):
    return lax.dot_general(
        left,
        right,
        (((left_dim,), (right_dim,)), ((), ())),
        precision=PRECISION,
        preferred_element_type=jnp.float32,
    )


def per_device(
    inverse,
    owner,
    struct_parent,
    struct_child,
    panel_parent,
    panel_child,
    child_on_parent,
    dinv_parent,
    dinv_child,
):
    rows_dev = inverse.shape[0]
    nblocks = owner.shape[0]
    rows, cols = lax.axis_size("row"), lax.axis_size("col")
    ratio = rows // cols
    width = child_on_parent.shape[1]
    chunk = width // cols
    row_at = lax.axis_index("row")
    row_tiles = rows_dev // BLOCK_ROWS
    matches = owner[:, None] == jnp.arange(nblocks, dtype=jnp.int32)[None, :]
    live_parent = jnp.sum(jnp.where(matches, struct_parent[None, :], 0), axis=1)
    live_child = live_parent * jnp.sum(jnp.where(matches, struct_child[None, :], 0), axis=1)
    parent_rowblk = lax.dynamic_slice_in_dim(live_parent, row_at * row_tiles, row_tiles)
    child_rowblk = lax.dynamic_slice_in_dim(live_child, row_at * row_tiles, row_tiles)
    mask_parent = jnp.repeat(parent_rowblk.astype(jnp.float32), BLOCK_ROWS)
    mask_child = jnp.repeat(child_rowblk.astype(jnp.float32), BLOCK_ROWS)
    masked_parent = panel_parent * mask_parent[:, None]
    masked_child = panel_child * mask_child[:, None]

    swap = [
        ((ratio * a + k) * cols + b, (ratio * b + k) * cols + a)
        for a in range(cols)
        for b in range(cols)
        for k in range(ratio)
    ]

    def column_panel(tile):
        moved = lax.ppermute(tile, ("row", "col"), swap)
        got = lax.all_gather(moved, "row", axis=0, tiled=True)
        return got.reshape(cols, ratio * rows_dev, chunk)

    def region_term(panel):
        return contract(panel, inverse, 1, 1)

    term_parent = region_term(column_panel(masked_parent))
    term_child = region_term(column_panel(masked_child))
    parent_full = lax.all_gather(child_on_parent, "col", axis=0, tiled=True)
    full_parent = lax.all_gather(masked_parent, "col", axis=1, tiled=True)
    full_child = lax.all_gather(masked_child, "col", axis=1, tiled=True)

    lower = contract(parent_full, term_parent.reshape(width, rows_dev), 0, 0)
    term_both = term_child.reshape(width, rows_dev) - lower
    row_parent = (
        -lax.psum_scatter(
            term_parent.reshape(width, rows_dev), "col", scatter_dimension=0, tiled=True
        )
        * mask_parent[None, :]
    )
    row_child = (
        -lax.psum_scatter(term_both, "col", scatter_dimension=0, tiled=True) * mask_child[None, :]
    )
    sum_parent, sum_cross, sum_child = lax.psum(
        (
            contract(row_parent, full_parent, 1, 0),
            contract(row_parent, full_child, 1, 0),
            contract(row_child, full_child, 1, 0),
        ),
        "row",
    )
    inv_parent = dinv_parent - sum_parent
    inv_cross = -(sum_cross + contract(inv_parent, parent_full, 1, 0))
    cross_column = lax.all_to_all(inv_cross, "col", split_axis=1, concat_axis=0, tiled=True)
    inv_child = dinv_child - sum_child - contract(cross_column, parent_full, 0, 0)
    return (row_parent, inv_parent, row_child, inv_cross, inv_child)


def solution(mesh):
    return jax.shard_map(
        per_device,
        mesh=mesh,
        in_specs=(
            P("row", "col"),
            P(),
            P(),
            P(),
            P("row", "col"),
            P("row", "col"),
            P("col", None),
            P("col", None),
            P("col", None),
        ),
        out_specs=(
            P("col", "row"),
            P("col", None),
            P("col", "row"),
            P("col", None),
            P("col", None),
        ),
        check_vma=False,
    )
```

```python
import functools

import jax
import jax.numpy as jnp
from jax import lax
from jax.experimental import pallas as pl
from jax.experimental.pallas import tpu as pltpu
from jax.sharding import PartitionSpec as P

BLOCK_ROWS = 128
PRECISION = lax.Precision.HIGH


def contract(left, right, left_dim, right_dim):
    return lax.dot_general(
        left,
        right,
        (((left_dim,), (right_dim,)), ((), ())),
        precision=PRECISION,
        preferred_element_type=jnp.float32,
    )


def exchange_kernel(
    rows, cols, lp, lc, cop, gp, gc, fp, fc, hp,
    t_send, t_recv, z_send, z_recv, r_send, r_recv, f_send, f_recv, c_send, c_recv, l_sem,
):
    chips = rows // 2
    row, col = lax.axis_index("row"), lax.axis_index("col")
    chip, core = row // 2, row % 2
    other = chip * 2 + (1 - core)
    swap_row, swap_col = col * 2 + core, chip
    off_diagonal = chip != col
    chunk = lp.shape[1]
    part = cop.shape[0]
    half = part // 2

    def remote(src, dst, send, recv, to):
        return pltpu.make_async_remote_copy(
            src_ref=src, dst_ref=dst, send_sem=send, recv_sem=recv,
            device_id=to, device_id_type=pl.DeviceIdType.MESH,
        )

    def columns(ref, at):
        return ref.at[:, pl.ds(pl.multiple_of(at * chunk, 128), chunk)]

    def half_rows(ref, at, which):
        return ref.at[pl.ds(pl.multiple_of(at * part + which * half, 8), half)]

    def greet(to):
        pl.semaphore_signal(barrier, inc=1, device_id=to, device_id_type=pl.DeviceIdType.MESH)

    barrier = pltpu.get_barrier_semaphore()
    for j in range(1, cols):
        greet((row, (col + j) % cols))
    for j in range(1, chips):
        greet((((chip + j) % chips) * 2 + core, col))
    greet((other, col))
    pl.when(off_diagonal)(lambda: greet((swap_row, swap_col)))
    pl.semaphore_wait(barrier, cols - 1 + chips - 1 + 1 + off_diagonal.astype(jnp.int32))

    tiles, columns_out, fulls = (lp, lc), (gp, gc), (fp, fc)

    def swap(p):
        return remote(
            tiles[p], columns_out[p].at[swap_row], t_send.at[p], t_recv.at[p], (swap_row, swap_col)
        )

    def swap_local(p):
        return pltpu.make_async_copy(tiles[p], columns_out[p].at[row], l_sem.at[3 + p])

    for p in range(2):
        pl.when(off_diagonal)(lambda p=p: swap(p).start())
        pl.when(jnp.logical_not(off_diagonal))(lambda p=p: swap_local(p).start())

    locals_ = [pltpu.make_async_copy(tiles[p], columns(fulls[p], col), l_sem.at[p]) for p in range(2)]
    locals_.append(
        pltpu.make_async_copy(
            cop, hp.at[pl.ds(pl.multiple_of(col * part, 8), part)], l_sem.at[2]
        )
    )
    for copy in locals_:
        copy.start()

    def along_panel(p, j, at):
        return remote(
            tiles[p], columns(fulls[p], at), z_send.at[p, j], z_recv.at[p, j],
            (row, (col + j) % cols),
        )

    def along_block(j, at):
        return remote(
            cop.at[pl.ds(pl.multiple_of(core * half, 8), half)], half_rows(hp, at, core),
            z_send.at[2, j], z_recv.at[2, j], (row, (col + j) % cols),
        )

    for j in range(1, cols):
        along_block(j, col).start()
    for p in range(2):
        for j in range(1, cols):
            along_panel(p, j, col).start()

    def across(p, j, slot):
        return remote(
            columns_out[p].at[row], columns_out[p].at[slot], r_send.at[p, j], r_recv.at[p, j],
            (((chip + j) % chips) * 2 + core, col),
        )

    def hand(p, j, slot):
        return remote(
            columns_out[p].at[slot], columns_out[p].at[slot], f_send.at[p, j], f_recv.at[p, j],
            (other, col),
        )

    for p in range(2):
        pl.when(off_diagonal)(lambda p=p: swap(p).wait_recv())
        pl.when(jnp.logical_not(off_diagonal))(lambda p=p: swap_local(p).wait())
        for j in range(1, chips):
            across(p, j, row).start()
        hand(p, 0, row).start()
    for p in range(2):
        for j in range(1, chips):
            slot = ((chip - j + chips) % chips) * 2 + core
            across(p, j, slot).wait_recv()
            hand(p, j, slot).start()

    def hand_block(j, which):
        block = half_rows(hp, (col - j + cols) % cols, which)
        return remote(block, block, c_send.at[j], c_recv.at[j], (other, col))

    for j in range(1, cols):
        along_block(j, (col - j + cols) % cols).wait_recv()
        hand_block(j, core).start()
    for p in range(2):
        for j in range(1, cols):
            along_panel(p, j, (col - j + cols) % cols).wait_recv()
    for j in range(1, cols):
        hand_block(j, 1 - core).wait_recv()
        hand_block(j, core).wait_send()
        along_block(j, col).wait_send()
    for p in range(2):
        for j in range(1, cols):
            along_panel(p, j, col).wait_send()
        for j in range(chips):
            chip_from = (chip - j + chips) % chips
            hand(p, j, chip_from * 2 + (1 - core)).wait_recv()
            hand(p, j, chip_from * 2 + core).wait_send()
            if j:
                across(p, j, row).wait_send()
        pl.when(off_diagonal)(lambda p=p: swap(p).wait_send())
    for copy in locals_:
        copy.wait()


def exchange(lp, lc, cop, rows, cols):
    size, chunk = lp.shape
    part, width = cop.shape
    chips = rows // 2
    sem = pltpu.SemaphoreType.DMA
    shape = lambda *dims: jax.ShapeDtypeStruct(dims, jnp.float32)
    anywhere = pl.BlockSpec(memory_space=pl.ANY)
    return pl.pallas_call(
        functools.partial(exchange_kernel, rows, cols),
        out_shape=(
            shape(rows, size, chunk), shape(rows, size, chunk),
            shape(size, width), shape(size, width), shape(width, width),
        ),
        in_specs=[anywhere] * 3,
        out_specs=[anywhere] * 5,
        scratch_shapes=[
            sem((2,)), sem((2,)), sem((3, cols)), sem((3, cols)), sem((2, chips)), sem((2, chips)),
            sem((2, chips)), sem((2, chips)), sem((cols,)), sem((cols,)), sem((5,)),
        ],
        compiler_params=pltpu.CompilerParams(collective_id=0, has_side_effects=True),
    )(lp, lc, cop)


def per_device(
    inverse,
    owner,
    struct_parent,
    struct_child,
    panel_parent,
    panel_child,
    child_on_parent,
    dinv_parent,
    dinv_child,
):
    rows_dev = inverse.shape[0]
    nblocks = owner.shape[0]
    rows, cols = lax.axis_size("row"), lax.axis_size("col")
    ratio = rows // cols
    width = child_on_parent.shape[1]
    chunk = width // cols
    row_at = lax.axis_index("row")
    row_tiles = rows_dev // BLOCK_ROWS
    matches = owner[:, None] == jnp.arange(nblocks, dtype=jnp.int32)[None, :]
    live_parent = jnp.sum(jnp.where(matches, struct_parent[None, :], 0), axis=1)
    live_child = live_parent * jnp.sum(jnp.where(matches, struct_child[None, :], 0), axis=1)
    parent_rowblk = lax.dynamic_slice_in_dim(live_parent, row_at * row_tiles, row_tiles)
    child_rowblk = lax.dynamic_slice_in_dim(live_child, row_at * row_tiles, row_tiles)
    mask_parent = jnp.repeat(parent_rowblk.astype(jnp.float32), BLOCK_ROWS)
    mask_child = jnp.repeat(child_rowblk.astype(jnp.float32), BLOCK_ROWS)
    masked_parent = panel_parent * mask_parent[:, None]
    masked_child = panel_child * mask_child[:, None]

    column_parent, column_child, full_parent, full_child, parent_full = exchange(
        masked_parent, masked_child, child_on_parent, rows, cols
    )

    def region_term(panel):
        return contract(panel, inverse, 1, 1)

    term_parent = region_term(column_parent.reshape(cols, ratio * rows_dev, chunk))
    term_child = region_term(column_child.reshape(cols, ratio * rows_dev, chunk))
    lower = contract(parent_full, term_parent.reshape(width, rows_dev), 0, 0)
    term_both = term_child.reshape(width, rows_dev) - lower
    row_parent = (
        -lax.psum_scatter(
            term_parent.reshape(width, rows_dev), "col", scatter_dimension=0, tiled=True
        )
        * mask_parent[None, :]
    )
    row_child = (
        -lax.psum_scatter(term_both, "col", scatter_dimension=0, tiled=True) * mask_child[None, :]
    )
    sum_parent, sum_cross, sum_child = lax.psum(
        (
            contract(row_parent, full_parent, 1, 0),
            contract(row_parent, full_child, 1, 0),
            contract(row_child, full_child, 1, 0),
        ),
        "row",
    )
    inv_parent = dinv_parent - sum_parent
    inv_cross = -(sum_cross + contract(inv_parent, parent_full, 1, 0))
    cross_column = lax.all_to_all(inv_cross, "col", split_axis=1, concat_axis=0, tiled=True)
    inv_child = dinv_child - sum_child - contract(cross_column, parent_full, 0, 0)
    return (row_parent, inv_parent, row_child, inv_cross, inv_child)


def solution(mesh):
    return jax.shard_map(
        per_device,
        mesh=mesh,
        in_specs=(
            P("row", "col"),
            P(),
            P(),
            P(),
            P("row", "col"),
            P("row", "col"),
            P("col", None),
            P("col", None),
            P("col", None),
        ),
        out_specs=(
            P("col", "row"),
            P("col", None),
            P("col", "row"),
            P("col", None),
            P("col", None),
        ),
        check_vma=False,
    )
```
